32 devices in a mesh: ctx: 16 (over z, x, core), head: 2 (over y).
Axes of the slice: x: 2, y: 2, z: 4, core: 2. Of those that a mesh axis runs over, the one named last changes fastest.
Arguments:
- queries: bfloat16 [2, 16384, 128], P('head', 'ctx'), may hold values from -12 to 12
- key_rows: bfloat16 [2, 16384, 128], P('head', 'ctx'), may hold values from -12 to 12
- value_rows: bfloat16 [2, 16384, 128], P('head', 'ctx'), may hold values from -6 to 6
- cluster_ids: int32 [2, 16384, 1], P('head', 'ctx'), may hold values from 0 to 31; in each aligned block of 1024 rows (0 to 1023, 1024 to 2047, ..., all dimensions but the last counted through in order) at most 64 rows name the same one
- out_weight: bfloat16 [256, 2048], P(None, 'head'), may hold values from -0.375 to 0.375
Outputs:
- projected: bfloat16 [16384, 2048], P('ctx', 'head')
- centroids: float32 [2, 32, 128], P('head', 'ctx')
The draws below stay inside these ranges and needn't reach their ends.
Inputs may be any that keep to these rules, and one draw needn't show every extreme that they name: `cluster_ids`: in each head, the 1024 tokens of one index of ctx name no cluster more than 64 times, a bound that some block reaches.
All inputs are finite; a program needn't handle non-finite values.
Results may differ from the reference program's by a relative error of at most 0.0054.
Values may be sent and summed in bfloat16 or wider, within the bound.
A program may use at most 64 MiB of HBM per device.

```python
import math
import jax
import jax.numpy as jnp
import numpy as np
from jax import lax

TOK_DEV = 1024
DH = 128
CAP = 1024
OUTW = 2048
HEADS = 2
CLUSTERS = 32
TOKENS = 16384
N_CTX = 16


def drawn_rows(key, salt):
    rows = jax.random.normal(jax.random.fold_in(key, salt), (HEADS, TOKENS, DH), jnp.float32)
    return jnp.clip(rows, -4.0, 4.0).astype(jnp.bfloat16)


def draw_queries(key, part):
    return drawn_rows(key, 101)


def draw_key_rows(key, part):
    return drawn_rows(key, 211)


def block_levels(stream_key, shape, split, least, largest):
    factor_of, own = 1.0, jax.random.fold_in(stream_key, 6)
    for position, shards_of in split:
        steps = jnp.exp(jax.random.uniform(jax.random.fold_in(own, position), (shards_of,), jnp.float32, least / len(split), largest / len(split)))
        factor_of = factor_of * jnp.repeat(steps, shape[position] // shards_of).reshape([-1 if axis == position else 1 for axis in range(len(shape))])
    return factor_of


def routed_block(key, own, number, rows, count, top, bound, skew):
    ranking = jax.random.permutation(key, count)
    crowded, ordinary = shares(count, rows * top, bound, skew, True), shares(count, rows * top, bound, skew, False)
    places = jnp.arange(count)

    def named(lengths, turn):
        used = int((lengths > 0).sum())
        fixed = max(1, used // 4)
        shifted = fixed + (places - fixed + turn * (used - fixed)) % max(1, count - fixed)
        return jnp.zeros((count,), jnp.int32).at[ranking[jnp.where(places < fixed, places, shifted)]].set(jnp.asarray(lengths, jnp.int32))

    lengths = jnp.where(number % 4 == 0, named(crowded, number // 4), named(ordinary, number - number // 4 - 1))
    mixed = jax.random.permutation(jax.random.fold_in(own, 3), count)
    giver, receiver = mixed[0:count // 2 * 2:2], mixed[1:count // 2 * 2:2]
    slack = jnp.minimum(lengths[giver] - 1, bound - lengths[receiver]) // 2
    slack = jnp.where((giver == ranking[0]) | (receiver == ranking[0]) | (lengths[receiver] == 0), 0, jnp.maximum(slack, 0))
    shifted = jax.random.randint(jax.random.fold_in(own, 4), (count // 2,), 0, 1 << 20) % (slack + 1)
    lengths = lengths.at[giver].add(-shifted).at[receiver].add(shifted)
    items = jnp.searchsorted(jnp.cumsum(lengths), jnp.arange(rows * top), side="right").astype(jnp.int32)
    table = items.reshape(top, rows).T
    table = table[jax.random.permutation(jax.random.fold_in(own, 1), rows)]
    turn = jax.random.randint(jax.random.fold_in(own, 2), (rows, 1), 0, top)
    return jnp.take_along_axis(table, (jnp.arange(top)[None, :] + turn) % top, axis=1)


def shares(number_of, total, most, lean, full):
    loads = [(1 << 20) // math.isqrt(rank ** lean) + 1 for rank in range(1, number_of + 1)]
    largest = most if full else min(most, max(-(-total // number_of), total * loads[0] // sum(loads)))
    least = 1 if total - largest >= number_of - 1 else 0
    given, rest = [largest] + [least] * (number_of - 1), total - largest - least * (number_of - 1)
    while rest > 0:
        candidates = [i for i in range(1, number_of) if given[i] < largest] or [i for i in range(1, number_of) if given[i] < most]
        mass, left = sum([loads[i] for i in candidates]), rest
        for i in candidates:
            addition = min(most - given[i], max(1, left * loads[i] // mass), rest)
            given[i] = given[i] + addition
            rest = rest - addition
    return np.array(given)


def normal_values(own_key, shape, deviation, bound, split=(), held_as=jnp.bfloat16):
    array = deviation * jax.random.normal(own_key, shape, jnp.float32)
    if split:
        array = array * block_levels(own_key, shape, split, -0.22, 0.18)
    return jnp.clip(array, -bound, bound).astype(held_as)


def setup_inputs(seed: int = 0) -> dict:
    splits = jax.random.split(jax.random.key(seed), 6)
    queries = draw_queries(jax.random.fold_in(splits[5], 71), 0)
    key_rows = draw_key_rows(jax.random.fold_in(splits[5], 71), 0)
    value_rows = normal_values(splits[2], (HEADS, TOKENS, DH), 1.0, 6.0, ((0, 2), (1, 16)))
    cluster_ids_keys = jax.random.split(jax.random.fold_in(splits[3], 1), HEADS * TOKENS // TOK_DEV)
    cluster_ids_turns = jax.random.permutation(jax.random.fold_in(splits[3], 3), HEADS * TOKENS // TOK_DEV)
    cluster_ids = jax.vmap(lambda own, number: routed_block(jax.random.fold_in(splits[3], 2), own, number, TOK_DEV, CLUSTERS, 1, CAP // N_CTX, 2))(cluster_ids_keys, cluster_ids_turns).reshape((HEADS, TOKENS, 1))
    out_weight = normal_values(splits[4], (HEADS * DH, OUTW), (HEADS * DH) ** -0.5, 0.375, ((1, 2),))
    return {"queries": queries, "key_rows": key_rows, "value_rows": value_rows, "cluster_ids": cluster_ids, "out_weight": out_weight}


norm_eps = 1e-06

def ranks_of(group):
    length = group.shape[0]
    block = math.gcd(512, length)
    columns = jnp.arange(length, dtype=jnp.int32)

    def block_ranks(start):
        mine = lax.dynamic_slice_in_dim(group, start, block)
        positions = start + jnp.arange(block, dtype=jnp.int32)
        earlier = (mine[:, None] == group[None, :]) & (columns[None, :] < positions[:, None])
        return lax.optimization_barrier(jnp.sum(earlier.astype(jnp.int32), axis=1))
    starts = jnp.arange(length // block, dtype=jnp.int32) * block
    return lax.map(block_ranks, starts).reshape(length)

def unit_rows(values):
    values = values.astype(jnp.float32)
    return values * lax.rsqrt(lax.optimization_barrier(jnp.mean(values * values, axis=-1, keepdims=True)) + norm_eps)

def cluster_attention(block_q, block_k, block_v, valid):
    length = block_q.shape[0]
    scores = lax.dot_general(block_q, block_k, (((1,), (1,)), ((), ())), preferred_element_type=jnp.float32)
    scores = scores * jnp.float32(block_q.shape[1] ** (-0.5))
    slots = jnp.arange(length, dtype=jnp.int32)
    allowed = (slots[None, :] <= slots[:, None]) & ((valid[None, :] > 0) | (slots[None, :] == slots[:, None]))
    scores = jnp.where(allowed, scores, jnp.float32(-1e+30))
    highest = lax.optimization_barrier(jnp.max(scores, axis=1, keepdims=True))
    weights = jnp.exp(scores - highest)
    total = lax.optimization_barrier(jnp.sum(weights, axis=1, keepdims=True))
    mixed = jnp.dot(weights.astype(jnp.bfloat16), block_v, preferred_element_type=jnp.float32)
    return (mixed / total).astype(jnp.bfloat16)

def head_output(head_q, head_k, head_v, group):
    tokens = group.shape[0]
    per_device = tokens // N_CTX
    send = CAP // N_CTX
    rank = lax.map(ranks_of, group.reshape(N_CTX, per_device)).reshape(tokens)
    source = jnp.arange(tokens, dtype=jnp.int32) // per_device
    where_row = (group * CAP + source * send + rank).astype(jnp.int32)
    total_rows = CLUSTERS * CAP

    def placed_rows(values):
        return jnp.zeros((total_rows, values.shape[1]), values.dtype).at[where_row].set(values)
    buffer_q = placed_rows(head_q)
    buffer_k = placed_rows(head_k)
    buffer_v = placed_rows(head_v)
    valid = jnp.zeros((total_rows,), jnp.int32).at[where_row].set(1)

    def one_cluster(index):
        start = (index * CAP).astype(jnp.int32)
        return cluster_attention(lax.dynamic_slice_in_dim(buffer_q, start, CAP), lax.dynamic_slice_in_dim(buffer_k, start, CAP), lax.dynamic_slice_in_dim(buffer_v, start, CAP), lax.dynamic_slice_in_dim(valid, start, CAP))
    attended = lax.map(one_cluster, jnp.arange(CLUSTERS, dtype=jnp.int32))
    return attended.reshape(total_rows, head_q.shape[1])[where_row]

def reference(queries, key_rows, value_rows, cluster_ids, out_weight):
    attended_all = []
    centroid_all = []
    for head in range(HEADS):
        group = cluster_ids[head, :, 0]
        attended_all.append(head_output(queries[head], key_rows[head], value_rows[head], group))
        unit = unit_rows(queries[head]) + unit_rows(key_rows[head])
        sums = jax.ops.segment_sum(unit, group, num_segments=CLUSTERS)
        centroid_all.append(sums * lax.rsqrt(lax.optimization_barrier(jnp.mean(sums * sums, axis=-1, keepdims=True)) + norm_eps))
    joined = jnp.concatenate(attended_all, axis=1)
    joined = joined.reshape(N_CTX, TOK_DEV, HEADS * DH)

    def project_block(rows):
        return jnp.dot(rows, out_weight, preferred_element_type=jnp.float32).astype(jnp.bfloat16)
    projected = lax.map(project_block, joined).reshape(TOKENS, OUTW)
    centroids = jnp.stack(centroid_all, axis=0)
    return (projected, centroids)
```

```python
import functools

import jax
import jax.numpy as jnp
from jax import lax
from jax.experimental import pallas as pl
from jax.experimental.pallas import tpu as pltpu
from jax.sharding import PartitionSpec as P

CL_DEV = 2
CAP = 1024
QUARTERS = 4
CHUNKS = 4
EMPTY = 2.0**100
LOW = -1e30

norm_eps = 1e-06
MESH = pl.DeviceIdType.MESH


def dot_t(a, b):
    return lax.dot_general(a, b, (((1,), (1,)), ((), ())), preferred_element_type=jnp.float32)


def unit_rows(values):
    return values * lax.rsqrt(jnp.mean(values * values, axis=-1, keepdims=True) + norm_eps)


def slots_of(ids, clusters, send):
    tokens = ids.shape[1]
    step = min(256, tokens)
    names = lax.broadcasted_iota(jnp.int32, (clusters, step), 0)
    before = lax.broadcasted_iota(jnp.int32, (step, step), 0)
    after = lax.broadcasted_iota(jnp.int32, (step, step), 1)
    earlier = jnp.where(before < after, 1.0, 0.0).astype(jnp.bfloat16)
    carry = jnp.zeros((clusters, 1), jnp.float32)
    out = []
    for start in range(0, tokens, step):
        part = ids[:, start : start + step]
        named = jnp.where(names == part, 1.0, 0.0)
        count = jnp.dot(named.astype(jnp.bfloat16), earlier, preferred_element_type=jnp.float32)
        rank = jnp.sum(named * (count + carry), axis=0, keepdims=True)
        carry = carry + jnp.sum(named, axis=1, keepdims=True)
        out.append(part * send + rank.astype(jnp.int32))
    return jnp.concatenate(out, axis=1)


def kernel(n, heads, send, q_hbm, k_hbm, v_hbm, ids_ref, joined_ref, cent_ref,
           rows, msg, recv, asked, att, att_x, back, back_x, parts, parts_x, told, told_x, stat, stat_x,
           keys, bias, cols, held_sum, got_sum, acc,
           in_sem, f_send, f_recv, q_send, q_recv, b_send, b_recv, x_send, x_recv,
           t_send, t_recv, u_send, u_recv, h_send, h_recv, c_send, c_recv):
    tokens, width = q_hbm.shape[1], q_hbm.shape[2]
    half = n // 2
    part = n // QUARTERS
    zones = QUARTERS // 2
    block = part * send
    span = half * send
    pair = CL_DEV * send
    me = lax.axis_index("ctx")
    head = lax.axis_index("head")
    side = me // half
    pos = lax.rem(me, half)
    base = side * half
    upper = side == 1
    lower = side == 0

    loads = []
    for i, ref in enumerate((q_hbm, k_hbm, v_hbm)):
        load = pltpu.make_async_copy(ref.at[0], rows.at[:, i * width : (i + 1) * width], in_sem.at[i])
        load.start()
        loads.append(load)

    barrier = pltpu.get_barrier_semaphore()

    def greet(i, carry):
        pl.semaphore_signal(barrier, inc=1, device_id=(lax.rem(me + i, n), head), device_id_type=MESH)
        return carry

    lax.fori_loop(1, n, greet, 0)
    for i in range(1, heads):
        pl.semaphore_signal(barrier, inc=1, device_id=(me, lax.rem(head + i, heads)), device_id_type=MESH)

    slot_row = slots_of(ids_ref[...], CL_DEV * n, send)
    cols[...] = jnp.transpose(jnp.broadcast_to(slot_row, (128, tokens)))
    rows[:, 3 * width :] = jnp.ones((tokens, width), jnp.bfloat16)
    for load in loads:
        load.wait()

    place_r = lax.broadcasted_iota(jnp.int32, (block, tokens), 0)
    place_r = place_r + (place_r // send) * ((CL_DEV - 1) * send)

    def fill(j, z):
        first = (z * part * CL_DEV + j) * send
        place = jnp.where(place_r + first == slot_row, 1.0, 0.0).astype(jnp.bfloat16)
        placed = jnp.dot(place, rows[...], preferred_element_type=jnp.float32)
        held = placed[:, 3 * width :]
        new = jnp.concatenate(
            [
                placed[:, :width],
                jnp.where(held > 0.5, placed[:, width : 2 * width], EMPTY),
                placed[:, 2 * width : 3 * width],
            ],
            axis=1,
        ).astype(jnp.bfloat16)
        msg[j, pl.ds(z * part, part)] = new.reshape(part, send, 3 * width)

    def forward(j, d, source, target):
        return pltpu.make_async_remote_copy(
            src_ref=msg.at[j, d], dst_ref=recv.at[j, source], send_sem=f_send.at[j, d], recv_sem=f_recv.at[j, source],
            device_id=(target, head), device_id_type=MESH)

    def ask(j, d, source, target):
        return pltpu.make_async_remote_copy(
            src_ref=msg.at[j, d, :, pl.ds(0, width)], dst_ref=asked.at[j, source],
            send_sem=q_send.at[j, d], recv_sem=q_recv.at[j, source],
            device_id=(target, head), device_id_type=MESH)

    def ship(j, z):
        group = z // zones

        def one(i, carry):
            d = z * part + lax.rem(me + i, part)
            p = d - group * half

            @pl.when(upper)
            def _():
                ask(j, d, group * half + pos, p).start()

            @pl.when(p != pos)
            def _():
                forward(j, d, group * half + pos, base + p).start()

            return carry

        lax.fori_loop(0, part, one, 0)

    def turn(t):
        group = t // (CL_DEV * zones)
        rest = lax.rem(t, CL_DEV * zones)
        return rest // zones, group * zones + lax.rem(rest + pos // part, zones)

    fill(*turn(0))
    pl.semaphore_wait(barrier, n - 1 + heads - 1)

    def dispatch(t, carry):
        fill(*turn(t))
        ship(*turn(t - 1))
        return carry

    steps = CL_DEV * QUARTERS
    lax.fori_loop(1, steps, dispatch, 0)
    ship(*turn(steps - 1))
    for j in range(CL_DEV):
        for group in range(2):
            recv[j, group * half + pos] = msg[j, group * half + pos]

    def returned(j, s, owner, target):
        return pltpu.make_async_remote_copy(
            src_ref=att.at[j, s], dst_ref=back.at[owner, j], send_sem=b_send.at[j, s], recv_sem=b_recv.at[j, owner],
            device_id=(target, head), device_id_type=MESH)

    def answered(j, s, owner, target):
        return pltpu.make_async_remote_copy(
            src_ref=att_x.at[j, s], dst_ref=back_x.at[owner, j], send_sem=x_send.at[j, s], recv_sem=x_recv.at[j, owner],
            device_id=(target, head), device_id_type=MESH)

    def noted(s, owner, target):
        return pltpu.make_async_remote_copy(
            src_ref=told.at[s], dst_ref=stat.at[owner], send_sem=t_send.at[s], recv_sem=t_recv.at[owner],
            device_id=(target, head), device_id_type=MESH)

    def noted_x(s, owner, target):
        return pltpu.make_async_remote_copy(
            src_ref=told_x.at[s], dst_ref=stat_x.at[owner], send_sem=u_send.at[s], recv_sem=u_recv.at[owner],
            device_id=(target, head), device_id_type=MESH)

    tri_r = lax.broadcasted_iota(jnp.int32, (block, block), 0)
    tri_c = lax.broadcasted_iota(jnp.int32, (block, block), 1)
    causal = jnp.where(tri_c <= tri_r, 0.0, LOW)
    ones = jnp.ones((8, width), jnp.bfloat16)
    scale = jnp.float32(width ** (-0.5))
    lane = lax.broadcasted_iota(jnp.int32, (block, width), 1)

    def split(highest, total):
        level = highest + jnp.log(total)
        top = level.astype(jnp.bfloat16).astype(jnp.float32)
        rest = level - top
        mid = rest.astype(jnp.bfloat16).astype(jnp.float32)
        pieces = jnp.where(lane == 0, top, jnp.where(lane == 1, mid, jnp.where(lane == 2, rest - mid, 0.0)))
        return pieces.astype(jnp.bfloat16).reshape(part, send, width)

    per = 128 // pair

    def line_up(ref, out, group):
        line = dot_t(ones, ref[...].reshape(half * pair, width))
        for s in range(half):
            row = line[0:1, (s // per) * 128 : (s // per + 1) * 128]
            shift = (128 - (s % per) * pair) % 128
            out[group * half + s] = row if shift == 0 else pltpu.roll(row, shift, 1)

    def gather(picks, ref, group):
        return jnp.dot(picks, ref[group * half : (group + 1) * half].reshape(half * pair, width),
                       preferred_element_type=jnp.float32)

    chunk = tokens // CHUNKS
    slot_lane = lax.broadcasted_iota(jnp.int32, (1, half * pair), 1)

    def chosen(c, group, weight):
        column = cols[pl.ds(pl.multiple_of(c * chunk, chunk), chunk)]
        wide = jnp.concatenate([column] * (half * pair // 128), axis=1)
        return jnp.where(wide == slot_lane + group * half * pair, weight, 0.0).astype(jnp.bfloat16)

    def passed(i, c):
        at = (pl.ds(pl.multiple_of(c * chunk, chunk), chunk), pl.ds(pl.multiple_of(head * width, width), width))
        return pltpu.make_async_remote_copy(
            src_ref=joined_ref.at[at], dst_ref=joined_ref.at[at], send_sem=h_send.at[i - 1, c], recv_sem=h_recv.at[i - 1, c],
            device_id=(me, lax.rem(head + i, heads)), device_id_type=MESH)

    def lined(ref, group):
        lines = []
        for g in range(half // per):
            line = ref[group * half + g * per]
            for r in range(1, per):
                within = (lax.broadcasted_iota(jnp.int32, (1, 128), 1) // pair) == r
                line = jnp.where(within, pltpu.roll(ref[group * half + g * per + r], r * pair, 1), line)
            lines.append(line)
        return jnp.concatenate(lines, axis=1)

    def collect(group):
        def finish(c, total):
            at = pl.ds(pl.multiple_of(c * chunk, chunk), chunk)
            if group == 0:
                acc[at] = total
            else:
                joined_ref[at, pl.ds(pl.multiple_of(head * width, width), width)] = (acc[at] + total).astype(jnp.bfloat16)
                for i in range(1, heads):
                    passed(i, c).start()

        def wait_back(p, carry):
            @pl.when(p != pos)
            def _():
                for j in range(CL_DEV):
                    returned(j, group * half + p, group * half + p, base + p).wait_recv()

                @pl.when(upper)
                def _():
                    noted(group * half + p, group * half + p, base + p).wait_recv()

            @pl.when(upper)
            def _():
                for j in range(CL_DEV):
                    answered(j, group * half + p, group * half + p, p).wait_recv()
                noted_x(group * half + p, group * half + p, p).wait_recv()

            return carry

        lax.fori_loop(0, half, wait_back, 0)

        @pl.when(lower)
        def _():
            def step(c, carry):
                finish(c, gather(chosen(c, group, 1.0), back, group))
                return carry

            lax.fori_loop(0, CHUNKS, step, 0)

        @pl.when(upper)
        def _():
            ours, theirs = lined(stat, group), lined(stat_x, group)
            keep = 1.0 / (1.0 + jnp.exp(theirs - ours))
            add = 1.0 / (1.0 + jnp.exp(ours - theirs))

            def step(c, carry):
                finish(c, gather(chosen(c, group, keep), back, group) + gather(chosen(c, group, add), back_x, group))
                return carry

            lax.fori_loop(0, CHUNKS, step, 0)

    for group in range(2):
        for j in range(CL_DEV):
            sums = jnp.zeros((1, width), jnp.float32)
            for b in range(zones):
                first, last, far = group * half + b * part, group * half + (b + 1) * part, (b + 1) * block

                def arrived(s, carry):
                    @pl.when(s != group * half + pos)
                    def _():
                        forward(j, s, s, base + s - group * half).wait_recv()

                    return carry

                lax.fori_loop(first, last, arrived, 0)
                q = recv[j, first:last, :, :width].reshape(block, width)
                k32 = recv[j, first:last, :, width : 2 * width].reshape(block, width).astype(jnp.float32)
                vacant = k32 > 0.5 * EMPTY
                k32 = jnp.where(vacant, 0.0, k32)
                keys[b * block : far, :] = k32.astype(jnp.bfloat16)
                flags = dot_t(ones, jnp.where(vacant, 1.0, 0.0).astype(jnp.bfloat16))
                bias[:, b * block : far] = jnp.where(flags > 0.5, LOW, 0.0)
                scores = dot_t(q, keys[:far, :]) * scale + bias[0:1, :far]
                tail = scores[:, b * block :] + causal
                scores = tail if b == 0 else jnp.concatenate([scores[:, : b * block], tail], axis=1)
                highest = jnp.max(scores, axis=1, keepdims=True)
                weights = jnp.exp(scores - highest)
                total = jnp.sum(weights, axis=1, keepdims=True)
                v = recv[j, group * half : last, :, 2 * width :].reshape(far, width)
                mixed = jnp.dot(weights.astype(jnp.bfloat16), v, preferred_element_type=jnp.float32)
                att[j, first:last] = (mixed / total).astype(jnp.bfloat16).reshape(part, send, width)
                parts[b * part : (b + 1) * part, j] = split(highest, total)
                unit = unit_rows(q.astype(jnp.float32)) + unit_rows(k32)
                sums = sums + jnp.sum(unit, axis=0, keepdims=True)

                def give(s, carry):
                    @pl.when(s != group * half + pos)
                    def _():
                        returned(j, s, group * half + pos, base + s - group * half).start()

                    return carry

                lax.fori_loop(first, last, give, 0)
            back[group * half + pos, j] = att[j, group * half + pos]
            held_sum[group, j : j + 1, :] = sums

            @pl.when(lower)
            def _():
                for b in range(zones):
                    first, last = group * half + b * part, group * half + (b + 1) * part

                    def wait_ask(s, carry):
                        ask(j, s, s, half + s - group * half).wait_recv()
                        return carry

                    lax.fori_loop(first, last, wait_ask, 0)
                    q = asked[j, first:last].reshape(block, width)
                    scores = dot_t(q, keys[...]) * scale + bias[0:1, :]
                    highest = jnp.max(scores, axis=1, keepdims=True)
                    weights = jnp.exp(scores - highest)
                    total = jnp.sum(weights, axis=1, keepdims=True)
                    v = recv[j, group * half : (group + 1) * half, :, 2 * width :].reshape(span, width)
                    mixed = jnp.dot(weights.astype(jnp.bfloat16), v, preferred_element_type=jnp.float32)
                    att_x[j, first:last] = (mixed / total).astype(jnp.bfloat16).reshape(part, send, width)
                    parts_x[b * part : (b + 1) * part, j] = split(highest, total)

                    def give_x(s, carry):
                        answered(j, s, group * half + pos, half + s - group * half).start()
                        return carry

                    lax.fori_loop(first, last, give_x, 0)

        @pl.when(upper)
        def _():
            line_up(parts, told, group)

            def tell(s, carry):
                @pl.when(s != pos)
                def _():
                    noted(group * half + s, group * half + pos, half + s).start()

                return carry

            lax.fori_loop(0, half, tell, 0)
            stat[group * half + pos] = told[group * half + pos]

        @pl.when(lower)
        def _():
            line_up(parts_x, told_x, group)

            def tell(s, carry):
                noted_x(group * half + s, group * half + pos, half + s).start()
                return carry

            lax.fori_loop(0, half, tell, 0)

    other = 1 - side
    swap = pltpu.make_async_remote_copy(
        src_ref=held_sum.at[other], dst_ref=got_sum, send_sem=c_send, recv_sem=c_recv,
        device_id=(other * half + pos, head), device_id_type=MESH)
    swap.start()

    collect(0)
    collect(1)

    swap.wait()
    sums = held_sum[side] + got_sum[...]
    mean = jnp.mean(sums * sums, axis=-1, keepdims=True)
    cent_ref[...] = sums * lax.rsqrt(mean + norm_eps)

    for i in range(1, heads):
        for c in range(CHUNKS):
            passed(i, c).wait()

    def settle(p, carry):
        for group in range(2):
            d = group * half + p

            @pl.when(p != pos)
            def _():
                for j in range(CL_DEV):
                    forward(j, d, group * half + pos, base + p).wait_send()
                    returned(j, d, group * half + pos, base + p).wait_send()

                @pl.when(upper)
                def _():
                    noted(d, group * half + pos, base + p).wait_send()

            @pl.when(upper)
            def _():
                for j in range(CL_DEV):
                    ask(j, d, group * half + pos, p).wait_send()

            @pl.when(lower)
            def _():
                for j in range(CL_DEV):
                    answered(j, d, group * half + pos, half + p).wait_send()
                noted_x(d, group * half + pos, half + p).wait_send()

        return carry

    lax.fori_loop(0, half, settle, 0)


def shards(n, heads, queries, key_rows, value_rows, cluster_ids, out_weight):
    tokens, width = queries.shape[1], queries.shape[2]
    send = CAP // n
    half = n // 2
    bf16, f32 = jnp.bfloat16, jnp.float32
    dma = pltpu.SemaphoreType.DMA
    joined, centroids = pl.pallas_call(
        functools.partial(kernel, n, heads, send),
        out_shape=(
            jax.ShapeDtypeStruct((tokens, heads * width), bf16),
            jax.ShapeDtypeStruct((CL_DEV, width), f32),
        ),
        in_specs=[pl.BlockSpec(memory_space=pltpu.HBM)] * 3 + [pl.BlockSpec(memory_space=pltpu.VMEM)],
        out_specs=(pl.BlockSpec(memory_space=pltpu.VMEM), pl.BlockSpec(memory_space=pltpu.VMEM)),
        scratch_shapes=[
            pltpu.VMEM((tokens, 4 * width), bf16),
            pltpu.VMEM((CL_DEV, n, send, 3 * width), bf16),
            pltpu.VMEM((CL_DEV, n, send, 3 * width), bf16),
            pltpu.VMEM((CL_DEV, n, send, width), bf16),
            pltpu.VMEM((CL_DEV, n, send, width), bf16),
            pltpu.VMEM((CL_DEV, n, send, width), bf16),
            pltpu.VMEM((n, CL_DEV, send, width), bf16),
            pltpu.VMEM((n, CL_DEV, send, width), bf16),
            pltpu.VMEM((half, CL_DEV, send, width), bf16),
            pltpu.VMEM((half, CL_DEV, send, width), bf16),
            pltpu.VMEM((n, 1, 128), f32),
            pltpu.VMEM((n, 1, 128), f32),
            pltpu.VMEM((n, 1, 128), f32),
            pltpu.VMEM((n, 1, 128), f32),
            pltpu.VMEM((half * send, width), bf16),
            pltpu.VMEM((8, half * send), f32),
            pltpu.VMEM((tokens, 128), jnp.int32),
            pltpu.VMEM((2, CL_DEV, width), f32),
            pltpu.VMEM((CL_DEV, width), f32),
            pltpu.VMEM((tokens, width), f32),
            dma((3,)),
        ]
        + [dma((CL_DEV, n))] * 8
        + [dma((n,))] * 4
        + [dma((max(1, heads - 1), CHUNKS))] * 2
        + [dma, dma],
        compiler_params=pltpu.CompilerParams(
            collective_id=0, has_side_effects=True, vmem_limit_bytes=60000000
        ),
        name="route",
    )(queries, key_rows, value_rows, cluster_ids[0, :, 0][None, :])
    projected = jnp.dot(joined, out_weight, preferred_element_type=f32).astype(bf16)
    return (projected, centroids[None])


def solution(mesh):
    in_specs = (
        P("head", "ctx", None),
        P("head", "ctx", None),
        P("head", "ctx", None),
        P("head", "ctx", None),
        P(None, "head"),
    )
    out_specs = (P("ctx", "head"), P("head", "ctx", None))
    body = functools.partial(shards, mesh.shape["ctx"], mesh.shape["head"])
    return jax.shard_map(body, mesh=mesh, in_specs=in_specs, out_specs=out_specs, check_vma=False)
```

```python
import functools

import jax
import jax.numpy as jnp
from jax import lax
from jax.experimental import pallas as pl
from jax.experimental.pallas import tpu as pltpu
from jax.sharding import PartitionSpec as P

CL_DEV = 2
CAP = 1024
QUARTERS = 4
CHUNKS = 4
EMPTY = 2.0**100
LOW = -1e30

norm_eps = 1e-06
MESH = pl.DeviceIdType.MESH


def dot_t(a, b):
    return lax.dot_general(a, b, (((1,), (1,)), ((), ())), preferred_element_type=jnp.float32)


def unit_rows(values):
    return values * lax.rsqrt(jnp.mean(values * values, axis=-1, keepdims=True) + norm_eps)


def slots_of(ids, clusters, send):
    tokens = ids.shape[1]
    step = min(256, tokens)
    names = lax.broadcasted_iota(jnp.int32, (clusters, step), 0)
    before = lax.broadcasted_iota(jnp.int32, (step, step), 0)
    after = lax.broadcasted_iota(jnp.int32, (step, step), 1)
    earlier = jnp.where(before < after, 1.0, 0.0).astype(jnp.bfloat16)
    carry = jnp.zeros((clusters, 1), jnp.float32)
    out = []
    for start in range(0, tokens, step):
        part = ids[:, start : start + step]
        named = jnp.where(names == part, 1.0, 0.0)
        count = jnp.dot(named.astype(jnp.bfloat16), earlier, preferred_element_type=jnp.float32)
        rank = jnp.sum(named * (count + carry), axis=0, keepdims=True)
        carry = carry + jnp.sum(named, axis=1, keepdims=True)
        out.append(part * send + rank.astype(jnp.int32))
    return jnp.concatenate(out, axis=1)


def kernel(n, heads, send, q_hbm, k_hbm, v_hbm, ids_hbm, weight_hbm, joined_ref, sums_ref, weight_ref,
           ids_ref, rows, msg, recv, asked, att, att_x, back, back_x, parts, parts_x, told, told_x, stat, stat_x,
           keys, bias, cols, held_sum, got_sum, acc,
           in_sem, f_send, f_recv, q_send, q_recv, b_send, b_recv, x_send, x_recv,
           t_send, t_recv, u_send, u_recv, h_send, h_recv, c_send, c_recv):
    tokens, width = q_hbm.shape[1], q_hbm.shape[2]
    half = n // 2
    part = n // QUARTERS
    zones = QUARTERS // 2
    block = part * send
    span = half * send
    pair = CL_DEV * send
    me = lax.axis_index("ctx")
    head = lax.axis_index("head")
    side = me // half
    pos = lax.rem(me, half)
    base = side * half
    upper = side == 1
    lower = side == 0

    named = pltpu.make_async_copy(ids_hbm, ids_ref, in_sem.at[3])
    named.start()
    loads = []
    for i, ref in enumerate((q_hbm, k_hbm, v_hbm)):
        load = pltpu.make_async_copy(ref.at[0], rows.at[:, i * width : (i + 1) * width], in_sem.at[i])
        load.start()
        loads.append(load)

    keep_weight = pltpu.make_async_copy(weight_hbm, weight_ref, in_sem.at[4])
    keep_weight.start()

    barrier = pltpu.get_barrier_semaphore()

    def greet(i, carry):
        pl.semaphore_signal(barrier, inc=1, device_id=(lax.rem(me + i, n), head), device_id_type=MESH)
        return carry

    lax.fori_loop(1, n, greet, 0)
    for i in range(1, heads):
        pl.semaphore_signal(barrier, inc=1, device_id=(me, lax.rem(head + i, heads)), device_id_type=MESH)

    named.wait()
    slot_row = slots_of(ids_ref[...], CL_DEV * n, send)
    rows[:, 3 * width :] = jnp.ones((tokens, width), jnp.bfloat16)
    for load in loads:
        load.wait()

    place_r = lax.broadcasted_iota(jnp.int32, (block, tokens), 0)
    place_r = place_r + (place_r // send) * ((CL_DEV - 1) * send)

    def fill(j, z):
        first = (z * part * CL_DEV + j) * send
        place = jnp.where(place_r + first == slot_row, 1.0, 0.0).astype(jnp.bfloat16)
        placed = jnp.dot(place, rows[...], preferred_element_type=jnp.float32)
        held = placed[:, 3 * width :]
        new = jnp.concatenate(
            [
                placed[:, :width],
                jnp.where(held > 0.5, placed[:, width : 2 * width], EMPTY),
                placed[:, 2 * width : 3 * width],
            ],
            axis=1,
        ).astype(jnp.bfloat16)
        msg[j, pl.ds(z * part, part)] = new.reshape(part, send, 3 * width)

    def forward(j, d, source, target):
        return pltpu.make_async_remote_copy(
            src_ref=msg.at[j, d], dst_ref=recv.at[j, source], send_sem=f_send.at[j, d], recv_sem=f_recv.at[j, source],
            device_id=(target, head), device_id_type=MESH)

    def ask(j, d, source, target):
        return pltpu.make_async_remote_copy(
            src_ref=msg.at[j, d, :, pl.ds(0, width)], dst_ref=asked.at[j, source],
            send_sem=q_send.at[j, d], recv_sem=q_recv.at[j, source],
            device_id=(target, head), device_id_type=MESH)

    def ship(j, z):
        group = z // zones

        def one(i, carry):
            d = z * part + lax.rem(me + i, part)
            p = d - group * half

            @pl.when(upper)
            def _():
                ask(j, d, group * half + pos, p).start()

            @pl.when(p != pos)
            def _():
                forward(j, d, group * half + pos, base + p).start()

            return carry

        lax.fori_loop(0, part, one, 0)

    def turn(t):
        group = t // (CL_DEV * zones)
        rest = lax.rem(t, CL_DEV * zones)
        return rest // zones, group * zones + lax.rem(rest + pos // part, zones)

    fill(*turn(0))
    pl.semaphore_wait(barrier, n - 1 + heads - 1)
    ship(*turn(0))

    def dispatch(t, carry):
        fill(*turn(t))
        ship(*turn(t))
        return carry

    lax.fori_loop(1, CL_DEV * QUARTERS, dispatch, 0)
    cols[...] = jnp.transpose(jnp.broadcast_to(slot_row, (128, tokens)))
    for j in range(CL_DEV):
        for group in range(2):
            recv[j, group * half + pos] = msg[j, group * half + pos]

    def returned(j, s, owner, target):
        return pltpu.make_async_remote_copy(
            src_ref=att.at[j, s], dst_ref=back.at[owner, j], send_sem=b_send.at[j, s], recv_sem=b_recv.at[j, owner],
            device_id=(target, head), device_id_type=MESH)

    def answered(j, s, owner, target):
        return pltpu.make_async_remote_copy(
            src_ref=att_x.at[j, s], dst_ref=back_x.at[owner, j], send_sem=x_send.at[j, s], recv_sem=x_recv.at[j, owner],
            device_id=(target, head), device_id_type=MESH)

    def noted(s, owner, target):
        return pltpu.make_async_remote_copy(
            src_ref=told.at[s], dst_ref=stat.at[owner], send_sem=t_send.at[s], recv_sem=t_recv.at[owner],
            device_id=(target, head), device_id_type=MESH)

    def noted_x(s, owner, target):
        return pltpu.make_async_remote_copy(
            src_ref=told_x.at[s], dst_ref=stat_x.at[owner], send_sem=u_send.at[s], recv_sem=u_recv.at[owner],
            device_id=(target, head), device_id_type=MESH)

    tri_r = lax.broadcasted_iota(jnp.int32, (block, block), 0)
    tri_c = lax.broadcasted_iota(jnp.int32, (block, block), 1)
    causal = jnp.where(tri_c <= tri_r, 0.0, LOW)
    ones = jnp.ones((8, width), jnp.bfloat16)
    scale = jnp.float32(width ** (-0.5))
    lane = lax.broadcasted_iota(jnp.int32, (block, width), 1)

    def split(highest, total):
        level = highest + jnp.log(total)
        top = level.astype(jnp.bfloat16).astype(jnp.float32)
        rest = level - top
        mid = rest.astype(jnp.bfloat16).astype(jnp.float32)
        pieces = jnp.where(lane == 0, top, jnp.where(lane == 1, mid, jnp.where(lane == 2, rest - mid, 0.0)))
        return pieces.astype(jnp.bfloat16).reshape(part, send, width)

    per = 128 // pair

    def line_up(ref, out, group):
        line = dot_t(ones, ref[...].reshape(half * pair, width))
        for s in range(half):
            row = line[0:1, (s // per) * 128 : (s // per + 1) * 128]
            shift = (128 - (s % per) * pair) % 128
            out[group * half + s] = row if shift == 0 else pltpu.roll(row, shift, 1)

    def gather(picks, ref, group):
        return jnp.dot(picks, ref[group * half : (group + 1) * half].reshape(half * pair, width),
                       preferred_element_type=jnp.float32)

    chunk = tokens // CHUNKS
    slot_lane = lax.broadcasted_iota(jnp.int32, (1, half * pair), 1)

    def chosen(c, group, weight):
        column = cols[pl.ds(pl.multiple_of(c * chunk, chunk), chunk)]
        wide = jnp.concatenate([column] * (half * pair // 128), axis=1)
        return jnp.where(wide == slot_lane + group * half * pair, weight, 0.0).astype(jnp.bfloat16)

    def passed(i, c):
        at = (pl.ds(pl.multiple_of(c * chunk, chunk), chunk), pl.ds(pl.multiple_of(head * width, width), width))
        return pltpu.make_async_remote_copy(
            src_ref=joined_ref.at[at], dst_ref=joined_ref.at[at], send_sem=h_send.at[i - 1, c], recv_sem=h_recv.at[i - 1, c],
            device_id=(me, lax.rem(head + i, heads)), device_id_type=MESH)

    def lined(ref, group):
        lines = []
        for g in range(half // per):
            line = ref[group * half + g * per]
            for r in range(1, per):
                within = (lax.broadcasted_iota(jnp.int32, (1, 128), 1) // pair) == r
                line = jnp.where(within, pltpu.roll(ref[group * half + g * per + r], r * pair, 1), line)
            lines.append(line)
        return jnp.concatenate(lines, axis=1)

    def collect(group):
        def finish(c, total):
            at = pl.ds(pl.multiple_of(c * chunk, chunk), chunk)
            if group == 0:
                acc[at] = total
            else:
                joined_ref[at, pl.ds(pl.multiple_of(head * width, width), width)] = (acc[at] + total).astype(jnp.bfloat16)
                for i in range(1, heads):
                    passed(i, c).start()

        def wait_back(p, carry):
            @pl.when(p != pos)
            def _():
                for j in range(CL_DEV):
                    returned(j, group * half + p, group * half + p, base + p).wait_recv()

                @pl.when(upper)
                def _():
                    noted(group * half + p, group * half + p, base + p).wait_recv()

            @pl.when(upper)
            def _():
                for j in range(CL_DEV):
                    answered(j, group * half + p, group * half + p, p).wait_recv()
                noted_x(group * half + p, group * half + p, p).wait_recv()

            return carry

        lax.fori_loop(0, half, wait_back, 0)

        @pl.when(lower)
        def _():
            def step(c, carry):
                finish(c, gather(chosen(c, group, 1.0), back, group))
                return carry

            lax.fori_loop(0, CHUNKS, step, 0)

        @pl.when(upper)
        def _():
            ours, theirs = lined(stat, group), lined(stat_x, group)
            keep = 1.0 / (1.0 + jnp.exp(theirs - ours))
            add = 1.0 / (1.0 + jnp.exp(ours - theirs))

            def step(c, carry):
                finish(c, gather(chosen(c, group, keep), back, group) + gather(chosen(c, group, add), back_x, group))
                return carry

            lax.fori_loop(0, CHUNKS, step, 0)

    for group in range(2):
        for j in range(CL_DEV):
            sums = jnp.zeros((1, width), jnp.float32)
            for b in range(zones):
                first, last, far = group * half + b * part, group * half + (b + 1) * part, (b + 1) * block

                def arrived(s, carry):
                    @pl.when(s != group * half + pos)
                    def _():
                        forward(j, s, s, base + s - group * half).wait_recv()

                    return carry

                lax.fori_loop(first, last, arrived, 0)
                q = recv[j, first:last, :, :width].reshape(block, width)
                k32 = recv[j, first:last, :, width : 2 * width].reshape(block, width).astype(jnp.float32)
                vacant = k32 > 0.5 * EMPTY
                k32 = jnp.where(vacant, 0.0, k32)
                keys[b * block : far, :] = k32.astype(jnp.bfloat16)
                flags = dot_t(ones, jnp.where(vacant, 1.0, 0.0).astype(jnp.bfloat16))
                bias[:, b * block : far] = jnp.where(flags > 0.5, LOW, 0.0)
                scores = dot_t(q, keys[:far, :]) * scale + bias[0:1, :far]
                tail = scores[:, b * block :] + causal
                scores = tail if b == 0 else jnp.concatenate([scores[:, : b * block], tail], axis=1)
                highest = jnp.max(scores, axis=1, keepdims=True)
                weights = jnp.exp(scores - highest)
                total = jnp.sum(weights, axis=1, keepdims=True)
                v = recv[j, group * half : last, :, 2 * width :].reshape(far, width)
                mixed = jnp.dot(weights.astype(jnp.bfloat16), v, preferred_element_type=jnp.float32)
                att[j, first:last] = (mixed / total).astype(jnp.bfloat16).reshape(part, send, width)
                parts[b * part : (b + 1) * part, j] = split(highest, total)
                unit = unit_rows(q.astype(jnp.float32)) + unit_rows(k32)
                sums = sums + jnp.sum(unit, axis=0, keepdims=True)

                def give(s, carry):
                    @pl.when(s != group * half + pos)
                    def _():
                        returned(j, s, group * half + pos, base + s - group * half).start()

                    return carry

                lax.fori_loop(first, last, give, 0)
            back[group * half + pos, j] = att[j, group * half + pos]
            held_sum[group, j : j + 1, :] = sums

            @pl.when(lower)
            def _():
                for b in range(zones):
                    first, last = group * half + b * part, group * half + (b + 1) * part

                    def wait_ask(s, carry):
                        ask(j, s, s, half + s - group * half).wait_recv()
                        return carry

                    lax.fori_loop(first, last, wait_ask, 0)
                    q = asked[j, first:last].reshape(block, width)
                    scores = dot_t(q, keys[...]) * scale + bias[0:1, :]
                    highest = jnp.max(scores, axis=1, keepdims=True)
                    weights = jnp.exp(scores - highest)
                    total = jnp.sum(weights, axis=1, keepdims=True)
                    v = recv[j, group * half : (group + 1) * half, :, 2 * width :].reshape(span, width)
                    mixed = jnp.dot(weights.astype(jnp.bfloat16), v, preferred_element_type=jnp.float32)
                    att_x[j, first:last] = (mixed / total).astype(jnp.bfloat16).reshape(part, send, width)
                    parts_x[b * part : (b + 1) * part, j] = split(highest, total)

                    def give_x(s, carry):
                        answered(j, s, group * half + pos, half + s - group * half).start()
                        return carry

                    lax.fori_loop(first, last, give_x, 0)

        @pl.when(upper)
        def _():
            line_up(parts, told, group)

            def tell(s, carry):
                @pl.when(s != pos)
                def _():
                    noted(group * half + s, group * half + pos, half + s).start()

                return carry

            lax.fori_loop(0, half, tell, 0)
            stat[group * half + pos] = told[group * half + pos]

        @pl.when(lower)
        def _():
            line_up(parts_x, told_x, group)

            def tell(s, carry):
                noted_x(group * half + s, group * half + pos, half + s).start()
                return carry

            lax.fori_loop(0, half, tell, 0)

    other = 1 - side
    swap = pltpu.make_async_remote_copy(
        src_ref=held_sum.at[other], dst_ref=got_sum, send_sem=c_send, recv_sem=c_recv,
        device_id=(other * half + pos, head), device_id_type=MESH)
    swap.start()

    collect(0)
    collect(1)

    swap.wait()
    sums = held_sum[side] + got_sum[...]
    sums_ref[...] = sums
    keep_weight.wait()

    for i in range(1, heads):
        for c in range(CHUNKS):
            passed(i, c).wait()

    def settle(p, carry):
        for group in range(2):
            d = group * half + p

            @pl.when(p != pos)
            def _():
                for j in range(CL_DEV):
                    forward(j, d, group * half + pos, base + p).wait_send()
                    returned(j, d, group * half + pos, base + p).wait_send()

                @pl.when(upper)
                def _():
                    noted(d, group * half + pos, base + p).wait_send()

            @pl.when(upper)
            def _():
                for j in range(CL_DEV):
                    ask(j, d, group * half + pos, p).wait_send()

            @pl.when(lower)
            def _():
                for j in range(CL_DEV):
                    answered(j, d, group * half + pos, half + p).wait_send()
                noted_x(d, group * half + pos, half + p).wait_send()

        return carry

    lax.fori_loop(0, half, settle, 0)


def project_kernel(steps, joined_ref, weight_ref, sums_ref, out_hbm, cent_ref, out, sem):
    rows = joined_ref.shape[0] // steps
    copies = []
    for i in range(steps):
        at = slice(i * rows, (i + 1) * rows)
        out[at] = jnp.dot(joined_ref[at], weight_ref[...], preferred_element_type=jnp.float32).astype(jnp.bfloat16)
        copy = pltpu.make_async_copy(out.at[at], out_hbm.at[at], sem.at[i])
        copy.start()
        copies.append(copy)
    sums = sums_ref[...]
    mean = jnp.mean(sums * sums, axis=-1, keepdims=True)
    cent_ref[0] = sums * lax.rsqrt(mean + norm_eps)
    for copy in copies:
        copy.wait()


def project(joined, weight, sums, steps):
    tokens, columns = joined.shape[0], weight.shape[1]
    return pl.pallas_call(
        functools.partial(project_kernel, steps),
        out_shape=(
            jax.ShapeDtypeStruct((tokens, columns), jnp.bfloat16),
            jax.ShapeDtypeStruct((1,) + sums.shape, jnp.float32),
        ),
        in_specs=[pl.BlockSpec(memory_space=pltpu.VMEM)] * 3,
        out_specs=(pl.BlockSpec(memory_space=pltpu.HBM), pl.BlockSpec(memory_space=pltpu.VMEM)),
        scratch_shapes=[pltpu.VMEM((tokens, columns), jnp.bfloat16), pltpu.SemaphoreType.DMA((steps,))],
        compiler_params=pltpu.CompilerParams(vmem_limit_bytes=8000000),
        name="project",
    )(joined, weight, sums)


def shards(n, heads, queries, key_rows, value_rows, cluster_ids, out_weight):
    tokens, width = queries.shape[1], queries.shape[2]
    send = CAP // n
    half = n // 2
    bf16, f32 = jnp.bfloat16, jnp.float32
    dma = pltpu.SemaphoreType.DMA
    pinned = [pltpu.with_memory_space_constraint(x, pltpu.HBM)
              for x in (queries, key_rows, value_rows, cluster_ids[0, :, 0][None, :], out_weight)]
    joined, sums, weight = pl.pallas_call(
        functools.partial(kernel, n, heads, send),
        out_shape=(
            jax.ShapeDtypeStruct((tokens, heads * width), bf16),
            jax.ShapeDtypeStruct((CL_DEV, width), f32),
            jax.ShapeDtypeStruct(out_weight.shape, bf16),
        ),
        in_specs=[pl.BlockSpec(memory_space=pltpu.HBM)] * 5,
        out_specs=(pl.BlockSpec(memory_space=pltpu.VMEM),) * 3,
        scratch_shapes=[
            pltpu.VMEM((1, tokens), jnp.int32),
            pltpu.VMEM((tokens, 4 * width), bf16),
            pltpu.VMEM((CL_DEV, n, send, 3 * width), bf16),
            pltpu.VMEM((CL_DEV, n, send, 3 * width), bf16),
            pltpu.VMEM((CL_DEV, n, send, width), bf16),
            pltpu.VMEM((CL_DEV, n, send, width), bf16),
            pltpu.VMEM((CL_DEV, n, send, width), bf16),
            pltpu.VMEM((n, CL_DEV, send, width), bf16),
            pltpu.VMEM((n, CL_DEV, send, width), bf16),
            pltpu.VMEM((half, CL_DEV, send, width), bf16),
            pltpu.VMEM((half, CL_DEV, send, width), bf16),
            pltpu.VMEM((n, 1, 128), f32),
            pltpu.VMEM((n, 1, 128), f32),
            pltpu.VMEM((n, 1, 128), f32),
            pltpu.VMEM((n, 1, 128), f32),
            pltpu.VMEM((half * send, width), bf16),
            pltpu.VMEM((8, half * send), f32),
            pltpu.VMEM((tokens, 128), jnp.int32),
            pltpu.VMEM((2, CL_DEV, width), f32),
            pltpu.VMEM((CL_DEV, width), f32),
            pltpu.VMEM((tokens, width), f32),
            dma((5,)),
        ]
        + [dma((CL_DEV, n))] * 8
        + [dma((n,))] * 4
        + [dma((max(1, heads - 1), CHUNKS))] * 2
        + [dma, dma],
        compiler_params=pltpu.CompilerParams(
            collective_id=0, has_side_effects=True, vmem_limit_bytes=40000000
        ),
        name="route",
    )(*pinned)
    return project(joined, weight, sums, 4)


def solution(mesh):
    in_specs = (
        P("head", "ctx", None),
        P("head", "ctx", None),
        P("head", "ctx", None),
        P("head", "ctx", None),
        P(None, "head"),
    )
    out_specs = (P("ctx", "head"), P("head", "ctx", None))
    body = functools.partial(shards, mesh.shape["ctx"], mesh.shape["head"])
    return jax.shard_map(body, mesh=mesh, in_specs=in_specs, out_specs=out_specs, check_vma=False)
```

```python
import functools

import jax
import jax.numpy as jnp
from jax import lax
from jax.experimental import pallas as pl
from jax.experimental.pallas import tpu as pltpu
from jax.sharding import PartitionSpec as P

CL_DEV = 2
CAP = 1024
QUARTERS = 4
CHUNKS = 4
EMPTY = 2.0**100
LOW = -1e30

norm_eps = 1e-06
MESH = pl.DeviceIdType.MESH


def dot_t(a, b):
    return lax.dot_general(a, b, (((1,), (1,)), ((), ())), preferred_element_type=jnp.float32)


def unit_rows(values):
    return values * lax.rsqrt(jnp.mean(values * values, axis=-1, keepdims=True) + norm_eps)


def slots_of(ids, clusters, send):
    tokens = ids.shape[1]
    step = min(256, tokens)
    names = lax.broadcasted_iota(jnp.int32, (clusters, step), 0)
    before = lax.broadcasted_iota(jnp.int32, (step, step), 0)
    after = lax.broadcasted_iota(jnp.int32, (step, step), 1)
    earlier = jnp.where(before < after, 1.0, 0.0).astype(jnp.bfloat16)
    carry = jnp.zeros((clusters, 1), jnp.float32)
    out = []
    for start in range(0, tokens, step):
        part = ids[:, start : start + step]
        named = jnp.where(names == part, 1.0, 0.0)
        count = jnp.dot(named.astype(jnp.bfloat16), earlier, preferred_element_type=jnp.float32)
        rank = jnp.sum(named * (count + carry), axis=0, keepdims=True)
        carry = carry + jnp.sum(named, axis=1, keepdims=True)
        out.append(part * send + rank.astype(jnp.int32))
    return jnp.concatenate(out, axis=1)


def kernel(n, heads, send, q_hbm, k_hbm, v_hbm, ids_hbm, weight_hbm, joined_ref, sums_ref, weight_ref,
           ids_ref, rows, msg, recv, asked, att, att_x, back, back_x, parts, parts_x, told, told_x, stat, stat_x,
           keys, bias, cols, held_sum, got_sum, acc,
           in_sem, f_send, f_recv, q_send, q_recv, b_send, b_recv, x_send, x_recv,
           t_send, t_recv, u_send, u_recv, h_send, h_recv, c_send, c_recv):
    tokens, width = q_hbm.shape[1], q_hbm.shape[2]
    half = n // 2
    part = n // QUARTERS
    zones = QUARTERS // 2
    block = part * send
    span = half * send
    pair = CL_DEV * send
    me = lax.axis_index("ctx")
    head = lax.axis_index("head")
    side = me // half
    pos = lax.rem(me, half)
    base = side * half
    upper = side == 1
    lower = side == 0

    named = pltpu.make_async_copy(ids_hbm, ids_ref, in_sem.at[3])
    named.start()
    loads = []
    for i, ref in enumerate((q_hbm, k_hbm, v_hbm)):
        load = pltpu.make_async_copy(ref.at[0], rows.at[:, i * width : (i + 1) * width], in_sem.at[i])
        load.start()
        loads.append(load)

    keep_weight = pltpu.make_async_copy(weight_hbm, weight_ref, in_sem.at[4])
    keep_weight.start()

    barrier = pltpu.get_barrier_semaphore()

    def greet(i, carry):
        pl.semaphore_signal(barrier, inc=1, device_id=(lax.rem(me + i, n), head), device_id_type=MESH)
        return carry

    lax.fori_loop(1, n, greet, 0)
    for i in range(1, heads):
        pl.semaphore_signal(barrier, inc=1, device_id=(me, lax.rem(head + i, heads)), device_id_type=MESH)

    named.wait()
    slot_row = slots_of(ids_ref[...], CL_DEV * n, send)
    rows[:, 3 * width :] = jnp.ones((tokens, width), jnp.bfloat16)
    for load in loads:
        load.wait()

    place_r = lax.broadcasted_iota(jnp.int32, (block, tokens), 0)
    place_r = place_r + (place_r // send) * ((CL_DEV - 1) * send)

    def fill(j, z):
        first = (z * part * CL_DEV + j) * send
        place = jnp.where(place_r + first == slot_row, 1.0, 0.0).astype(jnp.bfloat16)
        placed = jnp.dot(place, rows[...], preferred_element_type=jnp.float32)
        held = placed[:, 3 * width :]
        pieces = (
            placed[:, :width],
            jnp.where(held > 0.5, placed[:, width : 2 * width], EMPTY),
            placed[:, 2 * width : 3 * width],
        )
        for i, piece in enumerate(pieces):
            msg[j, pl.ds(z * part, part), i] = piece.astype(jnp.bfloat16).reshape(part, send, width)

    def forward(j, d, source, target):
        return pltpu.make_async_remote_copy(
            src_ref=msg.at[j, d], dst_ref=recv.at[j, source], send_sem=f_send.at[j, d], recv_sem=f_recv.at[j, source],
            device_id=(target, head), device_id_type=MESH)

    def ask(j, d, source, target):
        return pltpu.make_async_remote_copy(
            src_ref=msg.at[j, d, 0], dst_ref=asked.at[j, source],
            send_sem=q_send.at[j, d], recv_sem=q_recv.at[j, source],
            device_id=(target, head), device_id_type=MESH)

    def ship(j, z):
        group = z // zones

        def one(i, carry):
            d = z * part + lax.rem(me + i, part)
            p = d - group * half

            @pl.when(upper)
            def _():
                ask(j, d, group * half + pos, p).start()

            @pl.when(p != pos)
            def _():
                forward(j, d, group * half + pos, base + p).start()

            return carry

        lax.fori_loop(0, part, one, 0)

    def turn(t):
        group = t // (CL_DEV * zones)
        rest = lax.rem(t, CL_DEV * zones)
        return rest // zones, group * zones + lax.rem(rest + 1 + pos // part, zones)

    fill(*turn(0))
    pl.semaphore_wait(barrier, n - 1 + heads - 1)
    ship(*turn(0))

    def dispatch(t, carry):
        fill(*turn(t))
        ship(*turn(t))
        return carry

    lax.fori_loop(1, CL_DEV * QUARTERS, dispatch, 0)
    cols[...] = jnp.transpose(jnp.broadcast_to(slot_row, (128, tokens)))
    for j in range(CL_DEV):
        for group in range(2):
            recv[j, group * half + pos] = msg[j, group * half + pos]

    def returned(j, s, owner, target):
        return pltpu.make_async_remote_copy(
            src_ref=att.at[j, s], dst_ref=back.at[owner, j], send_sem=b_send.at[j, s], recv_sem=b_recv.at[j, owner],
            device_id=(target, head), device_id_type=MESH)

    def answered(j, s, owner, target):
        return pltpu.make_async_remote_copy(
            src_ref=att_x.at[j, s], dst_ref=back_x.at[owner, j], send_sem=x_send.at[j, s], recv_sem=x_recv.at[j, owner],
            device_id=(target, head), device_id_type=MESH)

    def noted(s, owner, target):
        return pltpu.make_async_remote_copy(
            src_ref=told.at[s], dst_ref=stat.at[owner], send_sem=t_send.at[s], recv_sem=t_recv.at[owner],
            device_id=(target, head), device_id_type=MESH)

    def noted_x(s, owner, target):
        return pltpu.make_async_remote_copy(
            src_ref=told_x.at[s], dst_ref=stat_x.at[owner], send_sem=u_send.at[s], recv_sem=u_recv.at[owner],
            device_id=(target, head), device_id_type=MESH)

    tri_r = lax.broadcasted_iota(jnp.int32, (block, block), 0)
    tri_c = lax.broadcasted_iota(jnp.int32, (block, block), 1)
    causal = jnp.where(tri_c <= tri_r, 0.0, LOW)
    ones = jnp.ones((8, width), jnp.bfloat16)
    scale = jnp.float32(width ** (-0.5))
    lane = lax.broadcasted_iota(jnp.int32, (block, width), 1)

    def split(highest, total):
        level = highest + jnp.log(total)
        top = level.astype(jnp.bfloat16).astype(jnp.float32)
        rest = level - top
        mid = rest.astype(jnp.bfloat16).astype(jnp.float32)
        pieces = jnp.where(lane == 0, top, jnp.where(lane == 1, mid, jnp.where(lane == 2, rest - mid, 0.0)))
        return pieces.astype(jnp.bfloat16).reshape(part, send, width)

    per = 128 // pair

    def line_up(ref, out, group):
        line = dot_t(ones, ref[...].reshape(half * pair, width))
        for s in range(half):
            row = line[0:1, (s // per) * 128 : (s // per + 1) * 128]
            shift = (128 - (s % per) * pair) % 128
            out[group * half + s] = row if shift == 0 else pltpu.roll(row, shift, 1)

    def gather(picks, ref, group):
        return jnp.dot(picks, ref[group * half : (group + 1) * half].reshape(half * pair, width),
                       preferred_element_type=jnp.float32)

    chunk = tokens // CHUNKS
    slot_lane = lax.broadcasted_iota(jnp.int32, (1, half * pair), 1)

    def chosen(c, group, weight):
        column = cols[pl.ds(pl.multiple_of(c * chunk, chunk), chunk)]
        wide = jnp.concatenate([column] * (half * pair // 128), axis=1)
        return jnp.where(wide == slot_lane + group * half * pair, weight, 0.0).astype(jnp.bfloat16)

    def passed(i, c):
        at = (pl.ds(pl.multiple_of(c * chunk, chunk), chunk), pl.ds(pl.multiple_of(head * width, width), width))
        return pltpu.make_async_remote_copy(
            src_ref=joined_ref.at[at], dst_ref=joined_ref.at[at], send_sem=h_send.at[i - 1, c], recv_sem=h_recv.at[i - 1, c],
            device_id=(me, lax.rem(head + i, heads)), device_id_type=MESH)

    def lined(ref, group):
        lines = []
        for g in range(half // per):
            line = ref[group * half + g * per]
            for r in range(1, per):
                within = (lax.broadcasted_iota(jnp.int32, (1, 128), 1) // pair) == r
                line = jnp.where(within, pltpu.roll(ref[group * half + g * per + r], r * pair, 1), line)
            lines.append(line)
        return jnp.concatenate(lines, axis=1)

    def collect(group):
        def finish(c, total):
            at = pl.ds(pl.multiple_of(c * chunk, chunk), chunk)
            if group == 0:
                acc[at] = total
            else:
                joined_ref[at, pl.ds(pl.multiple_of(head * width, width), width)] = (acc[at] + total).astype(jnp.bfloat16)
                for i in range(1, heads):
                    passed(i, c).start()

        def wait_back(p, carry):
            @pl.when(p != pos)
            def _():
                for j in range(CL_DEV):
                    returned(j, group * half + p, group * half + p, base + p).wait_recv()

                @pl.when(upper)
                def _():
                    noted(group * half + p, group * half + p, base + p).wait_recv()

            @pl.when(upper)
            def _():
                for j in range(CL_DEV):
                    answered(j, group * half + p, group * half + p, p).wait_recv()
                noted_x(group * half + p, group * half + p, p).wait_recv()

            return carry

        lax.fori_loop(0, half, wait_back, 0)

        @pl.when(lower)
        def _():
            def step(c, carry):
                finish(c, gather(chosen(c, group, 1.0), back, group))
                return carry

            lax.fori_loop(0, CHUNKS, step, 0)

        @pl.when(upper)
        def _():
            ours, theirs = lined(stat, group), lined(stat_x, group)
            keep = 1.0 / (1.0 + jnp.exp(theirs - ours))
            add = 1.0 / (1.0 + jnp.exp(ours - theirs))

            def step(c, carry):
                finish(c, gather(chosen(c, group, keep), back, group) + gather(chosen(c, group, add), back_x, group))
                return carry

            lax.fori_loop(0, CHUNKS, step, 0)

    for group in range(2):
        for j in range(CL_DEV):
            sums = jnp.zeros((1, width), jnp.float32)
            for b in range(zones):
                first, last, far = group * half + b * part, group * half + (b + 1) * part, (b + 1) * block

                def arrived(s, carry):
                    @pl.when(s != group * half + pos)
                    def _():
                        forward(j, s, s, base + s - group * half).wait_recv()

                    return carry

                lax.fori_loop(first, last, arrived, 0)
                q = recv[j, first:last, 0].reshape(block, width)
                k32 = recv[j, first:last, 1].reshape(block, width).astype(jnp.float32)
                vacant = k32 > 0.5 * EMPTY
                k32 = jnp.where(vacant, 0.0, k32)
                keys[b * block : far, :] = k32.astype(jnp.bfloat16)
                flags = dot_t(ones, jnp.where(vacant, 1.0, 0.0).astype(jnp.bfloat16))
                bias[:, b * block : far] = jnp.where(flags > 0.5, LOW, 0.0)
                scores = dot_t(q, keys[:far, :]) * scale + bias[0:1, :far]
                tail = scores[:, b * block :] + causal
                scores = tail if b == 0 else jnp.concatenate([scores[:, : b * block], tail], axis=1)
                highest = jnp.max(scores, axis=1, keepdims=True)
                weights = jnp.exp(scores - highest)
                total = jnp.sum(weights, axis=1, keepdims=True)
                v = recv[j, group * half : last, 2].reshape(far, width)
                mixed = jnp.dot(weights.astype(jnp.bfloat16), v, preferred_element_type=jnp.float32)
                att[j, first:last] = (mixed / total).astype(jnp.bfloat16).reshape(part, send, width)
                parts[b * part : (b + 1) * part, j] = split(highest, total)
                unit = unit_rows(q.astype(jnp.float32)) + unit_rows(k32)
                sums = sums + jnp.sum(unit, axis=0, keepdims=True)

                def give(s, carry):
                    @pl.when(s != group * half + pos)
                    def _():
                        returned(j, s, group * half + pos, base + s - group * half).start()

                    return carry

                lax.fori_loop(first, last, give, 0)
            back[group * half + pos, j] = att[j, group * half + pos]
            held_sum[group, j : j + 1, :] = sums

            @pl.when(lower)
            def _():
                for b in range(zones):
                    first, last = group * half + b * part, group * half + (b + 1) * part

                    def wait_ask(s, carry):
                        ask(j, s, s, half + s - group * half).wait_recv()
                        return carry

                    lax.fori_loop(first, last, wait_ask, 0)
                    q = asked[j, first:last].reshape(block, width)
                    scores = dot_t(q, keys[...]) * scale + bias[0:1, :]
                    highest = jnp.max(scores, axis=1, keepdims=True)
                    weights = jnp.exp(scores - highest)
                    total = jnp.sum(weights, axis=1, keepdims=True)
                    v = recv[j, group * half : (group + 1) * half, 2].reshape(span, width)
                    mixed = jnp.dot(weights.astype(jnp.bfloat16), v, preferred_element_type=jnp.float32)
                    att_x[j, first:last] = (mixed / total).astype(jnp.bfloat16).reshape(part, send, width)
                    parts_x[b * part : (b + 1) * part, j] = split(highest, total)

                    def give_x(s, carry):
                        answered(j, s, group * half + pos, half + s - group * half).start()
                        return carry

                    lax.fori_loop(first, last, give_x, 0)

        @pl.when(upper)
        def _():
            line_up(parts, told, group)

            def tell(s, carry):
                @pl.when(s != pos)
                def _():
                    noted(group * half + s, group * half + pos, half + s).start()

                return carry

            lax.fori_loop(0, half, tell, 0)
            stat[group * half + pos] = told[group * half + pos]

        @pl.when(lower)
        def _():
            line_up(parts_x, told_x, group)

            def tell(s, carry):
                noted_x(group * half + s, group * half + pos, half + s).start()
                return carry

            lax.fori_loop(0, half, tell, 0)

    other = 1 - side
    swap = pltpu.make_async_remote_copy(
        src_ref=held_sum.at[other], dst_ref=got_sum, send_sem=c_send, recv_sem=c_recv,
        device_id=(other * half + pos, head), device_id_type=MESH)
    swap.start()

    collect(0)
    collect(1)

    swap.wait()
    sums = held_sum[side] + got_sum[...]
    sums_ref[...] = sums
    keep_weight.wait()

    for i in range(1, heads):
        for c in range(CHUNKS):
            passed(i, c).wait()

    def settle(p, carry):
        for group in range(2):
            d = group * half + p

            @pl.when(p != pos)
            def _():
                for j in range(CL_DEV):
                    forward(j, d, group * half + pos, base + p).wait_send()
                    returned(j, d, group * half + pos, base + p).wait_send()

                @pl.when(upper)
                def _():
                    noted(d, group * half + pos, base + p).wait_send()

            @pl.when(upper)
            def _():
                for j in range(CL_DEV):
                    ask(j, d, group * half + pos, p).wait_send()

            @pl.when(lower)
            def _():
                for j in range(CL_DEV):
                    answered(j, d, group * half + pos, half + p).wait_send()
                noted_x(d, group * half + pos, half + p).wait_send()

        return carry

    lax.fori_loop(0, half, settle, 0)


def project_kernel(steps, joined_ref, weight_ref, sums_ref, out_hbm, cent_hbm, out, cent, sem):
    rows = joined_ref.shape[0] // steps
    sums = sums_ref[...]
    mean = jnp.mean(sums * sums, axis=-1, keepdims=True)
    cent[0] = sums * lax.rsqrt(mean + norm_eps)
    copies = [pltpu.make_async_copy(cent, cent_hbm, sem.at[steps])]
    copies[0].start()
    for i in range(steps):
        at = slice(i * rows, (i + 1) * rows)
        out[at] = jnp.dot(joined_ref[at], weight_ref[...], preferred_element_type=jnp.float32).astype(jnp.bfloat16)
        copy = pltpu.make_async_copy(out.at[at], out_hbm.at[at], sem.at[i])
        copy.start()
        copies.append(copy)
    for copy in copies:
        copy.wait()


def project(joined, weight, sums, steps):
    tokens, columns = joined.shape[0], weight.shape[1]
    return pl.pallas_call(
        functools.partial(project_kernel, steps),
        out_shape=(
            jax.ShapeDtypeStruct((tokens, columns), jnp.bfloat16),
            jax.ShapeDtypeStruct((1,) + sums.shape, jnp.float32),
        ),
        in_specs=[pl.BlockSpec(memory_space=pltpu.VMEM)] * 3,
        out_specs=(pl.BlockSpec(memory_space=pltpu.HBM),) * 2,
        scratch_shapes=[
            pltpu.VMEM((tokens, columns), jnp.bfloat16),
            pltpu.VMEM((1,) + sums.shape, jnp.float32),
            pltpu.SemaphoreType.DMA((steps + 1,)),
        ],
        compiler_params=pltpu.CompilerParams(vmem_limit_bytes=8000000),
        name="project",
    )(joined, weight, sums)


def shards(n, heads, queries, key_rows, value_rows, cluster_ids, out_weight):
    tokens, width = queries.shape[1], queries.shape[2]
    send = CAP // n
    half = n // 2
    bf16, f32 = jnp.bfloat16, jnp.float32
    dma = pltpu.SemaphoreType.DMA
    pinned = [pltpu.with_memory_space_constraint(x, pltpu.HBM)
              for x in (queries, key_rows, value_rows, cluster_ids[0, :, 0][None, :], out_weight)]
    joined, sums, weight = pl.pallas_call(
        functools.partial(kernel, n, heads, send),
        out_shape=(
            jax.ShapeDtypeStruct((tokens, heads * width), bf16),
            jax.ShapeDtypeStruct((CL_DEV, width), f32),
            jax.ShapeDtypeStruct(out_weight.shape, bf16),
        ),
        in_specs=[pl.BlockSpec(memory_space=pltpu.HBM)] * 5,
        out_specs=(pl.BlockSpec(memory_space=pltpu.VMEM),) * 3,
        scratch_shapes=[
            pltpu.VMEM((1, tokens), jnp.int32),
            pltpu.VMEM((tokens, 4 * width), bf16),
            pltpu.VMEM((CL_DEV, n, 3, send, width), bf16),
            pltpu.VMEM((CL_DEV, n, 3, send, width), bf16),
            pltpu.VMEM((CL_DEV, n, send, width), bf16),
            pltpu.VMEM((CL_DEV, n, send, width), bf16),
            pltpu.VMEM((CL_DEV, n, send, width), bf16),
            pltpu.VMEM((n, CL_DEV, send, width), bf16),
            pltpu.VMEM((n, CL_DEV, send, width), bf16),
            pltpu.VMEM((half, CL_DEV, send, width), bf16),
            pltpu.VMEM((half, CL_DEV, send, width), bf16),
            pltpu.VMEM((n, 1, 128), f32),
            pltpu.VMEM((n, 1, 128), f32),
            pltpu.VMEM((n, 1, 128), f32),
            pltpu.VMEM((n, 1, 128), f32),
            pltpu.VMEM((half * send, width), bf16),
            pltpu.VMEM((8, half * send), f32),
            pltpu.VMEM((tokens, 128), jnp.int32),
            pltpu.VMEM((2, CL_DEV, width), f32),
            pltpu.VMEM((CL_DEV, width), f32),
            pltpu.VMEM((tokens, width), f32),
            dma((5,)),
        ]
        + [dma((CL_DEV, n))] * 8
        + [dma((n,))] * 4
        + [dma((max(1, heads - 1), CHUNKS))] * 2
        + [dma, dma],
        compiler_params=pltpu.CompilerParams(
            collective_id=0, has_side_effects=True, vmem_limit_bytes=40000000
        ),
        name="route",
    )(*pinned)
    return project(joined, weight, sums, 4)


def solution(mesh):
    in_specs = (
        P("head", "ctx", None),
        P("head", "ctx", None),
        P("head", "ctx", None),
        P("head", "ctx", None),
        P(None, "head"),
    )
    out_specs = (P("ctx", "head"), P("head", "ctx", None))
    body = functools.partial(shards, mesh.shape["ctx"], mesh.shape["head"])
    return jax.shard_map(body, mesh=mesh, in_specs=in_specs, out_specs=out_specs, check_vma=False)
```

```python
import functools

import jax
import jax.numpy as jnp
from jax import lax
from jax.experimental import pallas as pl
from jax.experimental.pallas import tpu as pltpu
from jax.sharding import PartitionSpec as P

CL_DEV = 2
CAP = 1024
QUARTERS = 4
CHUNKS = 4
EMPTY = 2.0**100
LOW = -1e30

norm_eps = 1e-06
MESH = pl.DeviceIdType.MESH


def dot_t(a, b):
    return lax.dot_general(a, b, (((1,), (1,)), ((), ())), preferred_element_type=jnp.float32)


def unit_rows(values):
    return values * lax.rsqrt(jnp.mean(values * values, axis=-1, keepdims=True) + norm_eps)


def slots_of(ids, clusters, send):
    tokens = ids.shape[1]
    step = min(256, tokens)
    names = lax.broadcasted_iota(jnp.int32, (clusters, step), 0)
    before = lax.broadcasted_iota(jnp.int32, (step, step), 0)
    after = lax.broadcasted_iota(jnp.int32, (step, step), 1)
    earlier = jnp.where(before < after, 1.0, 0.0).astype(jnp.bfloat16)
    carry = jnp.zeros((clusters, 1), jnp.float32)
    out = []
    for start in range(0, tokens, step):
        part = ids[:, start : start + step]
        named = jnp.where(names == part, 1.0, 0.0)
        count = jnp.dot(named.astype(jnp.bfloat16), earlier, preferred_element_type=jnp.float32)
        rank = jnp.sum(named * (count + carry), axis=0, keepdims=True)
        carry = carry + jnp.sum(named, axis=1, keepdims=True)
        out.append(part * send + rank.astype(jnp.int32))
    return jnp.concatenate(out, axis=1)


def kernel(n, heads, send, q_hbm, k_hbm, v_hbm, ids_hbm, weight_hbm, joined_ref, sums_ref, weight_ref,
           ids_ref, rows, msg, recv, asked, att, att_x, back, back_x, parts, parts_x, told, told_x, stat, stat_x,
           lent, keys, bias, keys_x, bias_x, cols, held_sum, got_sum, acc,
           in_sem, f_send, f_recv, q_send, q_recv, b_send, b_recv, x_send, x_recv,
           t_send, t_recv, u_send, u_recv, h_send, h_recv, c_send, c_recv):
    tokens, width = q_hbm.shape[1], q_hbm.shape[2]
    half = n // 2
    part = n // QUARTERS
    zones = QUARTERS // 2
    block = part * send
    span = half * send
    pair = CL_DEV * send
    me = lax.axis_index("ctx")
    head = lax.axis_index("head")
    side = me // half
    pos = lax.rem(me, half)
    base = side * half
    upper = side == 1
    lower = side == 0

    named = pltpu.make_async_copy(ids_hbm, ids_ref, in_sem.at[3])
    named.start()
    loads = []
    for i, ref in enumerate((q_hbm, k_hbm, v_hbm)):
        load = pltpu.make_async_copy(ref.at[0], rows.at[:, i * width : (i + 1) * width], in_sem.at[i])
        load.start()
        loads.append(load)

    keep_weight = pltpu.make_async_copy(weight_hbm, weight_ref, in_sem.at[4])
    keep_weight.start()

    barrier = pltpu.get_barrier_semaphore()

    def greet(i, carry):
        pl.semaphore_signal(barrier, inc=1, device_id=(lax.rem(me + i, n), head), device_id_type=MESH)
        return carry

    lax.fori_loop(1, n, greet, 0)
    for i in range(1, heads):
        pl.semaphore_signal(barrier, inc=1, device_id=(me, lax.rem(head + i, heads)), device_id_type=MESH)

    named.wait()
    slot_row = slots_of(ids_ref[...], CL_DEV * n, send)
    rows[:, 3 * width :] = jnp.ones((tokens, width), jnp.bfloat16)
    for load in loads:
        load.wait()

    place_r = lax.broadcasted_iota(jnp.int32, (block, tokens), 0)
    place_r = place_r + (place_r // send) * ((CL_DEV - 1) * send)

    def fill(j, z):
        first = (z * part * CL_DEV + j) * send
        place = jnp.where(place_r + first == slot_row, 1.0, 0.0).astype(jnp.bfloat16)
        placed = jnp.dot(place, rows[...], preferred_element_type=jnp.float32)
        held = placed[:, 3 * width :]
        pieces = (
            placed[:, :width],
            jnp.where(held > 0.5, placed[:, width : 2 * width], EMPTY),
            placed[:, 2 * width : 3 * width],
        )
        for i, piece in enumerate(pieces):
            msg[j, pl.ds(z * part, part), i] = piece.astype(jnp.bfloat16).reshape(part, send, width)

    def forward(j, d, source, target):
        return pltpu.make_async_remote_copy(
            src_ref=msg.at[j, d], dst_ref=recv.at[j, source], send_sem=f_send.at[j, d], recv_sem=f_recv.at[j, source],
            device_id=(target, head), device_id_type=MESH)

    def ask(j, d, source, target):
        return pltpu.make_async_remote_copy(
            src_ref=msg.at[j, d, 0], dst_ref=asked.at[j, source],
            send_sem=q_send.at[j, d], recv_sem=q_recv.at[j, source],
            device_id=(target, head), device_id_type=MESH)

    def lend(d, source, target):
        return pltpu.make_async_remote_copy(
            src_ref=msg.at[CL_DEV - 1, d, pl.ds(1, 2)], dst_ref=lent.at[source],
            send_sem=q_send.at[CL_DEV - 1, d], recv_sem=q_recv.at[CL_DEV - 1, half + source],
            device_id=(target, head), device_id_type=MESH)

    def ship(j, z):
        group = z // zones
        final = jnp.logical_and(group == 1, j == CL_DEV - 1)

        def one(i, carry):
            d = z * part + lax.rem(me + i, part)
            p = d - group * half

            @pl.when(jnp.logical_and(upper, jnp.logical_not(final)))
            def _():
                ask(j, d, group * half + pos, p).start()

            @pl.when(jnp.logical_and(lower, final))
            def _():
                lend(d, pos, half + p).start()

            @pl.when(p != pos)
            def _():
                forward(j, d, group * half + pos, base + p).start()

            return carry

        lax.fori_loop(0, part, one, 0)

    def turn(t):
        group = t // (CL_DEV * zones)
        rest = lax.rem(t, CL_DEV * zones)
        return rest // zones, group * zones + lax.rem(rest + 1 + pos // part, zones)

    fill(*turn(0))
    pl.semaphore_wait(barrier, n - 1 + heads - 1)
    ship(*turn(0))

    def dispatch(t, carry):
        fill(*turn(t))
        ship(*turn(t))
        return carry

    lax.fori_loop(1, CL_DEV * QUARTERS, dispatch, 0)
    cols[...] = jnp.transpose(jnp.broadcast_to(slot_row, (128, tokens)))
    back_x[half:, CL_DEV - 1] = jnp.zeros((half, send, width), jnp.bfloat16)
    for j in range(CL_DEV):
        for group in range(2):
            recv[j, group * half + pos] = msg[j, group * half + pos]

    def returned(j, s, owner, target):
        return pltpu.make_async_remote_copy(
            src_ref=att.at[j, s], dst_ref=back.at[owner, j], send_sem=b_send.at[j, s], recv_sem=b_recv.at[j, owner],
            device_id=(target, head), device_id_type=MESH)

    def answered(j, s, owner, target):
        return pltpu.make_async_remote_copy(
            src_ref=att_x.at[j, s], dst_ref=back_x.at[owner, j], send_sem=x_send.at[j, s], recv_sem=x_recv.at[j, owner],
            device_id=(target, head), device_id_type=MESH)

    def noted(s, owner, target):
        return pltpu.make_async_remote_copy(
            src_ref=told.at[s], dst_ref=stat.at[owner], send_sem=t_send.at[s], recv_sem=t_recv.at[owner],
            device_id=(target, head), device_id_type=MESH)

    def noted_x(s, owner, target):
        return pltpu.make_async_remote_copy(
            src_ref=told_x.at[s], dst_ref=stat_x.at[owner], send_sem=u_send.at[s], recv_sem=u_recv.at[owner],
            device_id=(target, head), device_id_type=MESH)

    tri_r = lax.broadcasted_iota(jnp.int32, (block, block), 0)
    tri_c = lax.broadcasted_iota(jnp.int32, (block, block), 1)
    causal = jnp.where(tri_c <= tri_r, 0.0, LOW)
    ones = jnp.ones((8, width), jnp.bfloat16)
    scale = jnp.float32(width ** (-0.5))
    lane = lax.broadcasted_iota(jnp.int32, (block, width), 1)

    def split(highest, total):
        level = highest + jnp.log(total)
        top = level.astype(jnp.bfloat16).astype(jnp.float32)
        rest = level - top
        mid = rest.astype(jnp.bfloat16).astype(jnp.float32)
        pieces = jnp.where(lane == 0, top, jnp.where(lane == 1, mid, jnp.where(lane == 2, rest - mid, 0.0)))
        return pieces.astype(jnp.bfloat16).reshape(part, send, width)

    per = 128 // pair

    def line_up(ref, out, group):
        line = dot_t(ones, ref[...].reshape(half * pair, width))
        for s in range(half):
            row = line[0:1, (s // per) * 128 : (s // per + 1) * 128]
            shift = (128 - (s % per) * pair) % 128
            out[group * half + s] = row if shift == 0 else pltpu.roll(row, shift, 1)

    def gather(picks, ref, group):
        return jnp.dot(picks, ref[group * half : (group + 1) * half].reshape(half * pair, width),
                       preferred_element_type=jnp.float32)

    chunk = tokens // CHUNKS
    slot_lane = lax.broadcasted_iota(jnp.int32, (1, half * pair), 1)

    def chosen(c, group, weight):
        column = cols[pl.ds(pl.multiple_of(c * chunk, chunk), chunk)]
        wide = jnp.concatenate([column] * (half * pair // 128), axis=1)
        return jnp.where(wide == slot_lane + group * half * pair, weight, 0.0).astype(jnp.bfloat16)

    def passed(i, c):
        at = (pl.ds(pl.multiple_of(c * chunk, chunk), chunk), pl.ds(pl.multiple_of(head * width, width), width))
        return pltpu.make_async_remote_copy(
            src_ref=joined_ref.at[at], dst_ref=joined_ref.at[at], send_sem=h_send.at[i - 1, c], recv_sem=h_recv.at[i - 1, c],
            device_id=(me, lax.rem(head + i, heads)), device_id_type=MESH)

    def lined(ref, group):
        lines = []
        for g in range(half // per):
            line = ref[group * half + g * per]
            for r in range(1, per):
                within = (lax.broadcasted_iota(jnp.int32, (1, 128), 1) // pair) == r
                line = jnp.where(within, pltpu.roll(ref[group * half + g * per + r], r * pair, 1), line)
            lines.append(line)
        return jnp.concatenate(lines, axis=1)

    def collect(group):
        def finish(c, total):
            at = pl.ds(pl.multiple_of(c * chunk, chunk), chunk)
            if group == 0:
                acc[at] = total
            else:
                joined_ref[at, pl.ds(pl.multiple_of(head * width, width), width)] = (acc[at] + total).astype(jnp.bfloat16)
                for i in range(1, heads):
                    passed(i, c).start()

        def wait_back(p, carry):
            @pl.when(p != pos)
            def _():
                for j in range(CL_DEV):
                    returned(j, group * half + p, group * half + p, base + p).wait_recv()

                @pl.when(upper)
                def _():
                    noted(group * half + p, group * half + p, base + p).wait_recv()

            @pl.when(upper)
            def _():
                for j in range(CL_DEV - group):
                    answered(j, group * half + p, group * half + p, p).wait_recv()
                noted_x(group * half + p, group * half + p, p).wait_recv()

            return carry

        lax.fori_loop(0, half, wait_back, 0)

        @pl.when(lower)
        def _():
            def step(c, carry):
                finish(c, gather(chosen(c, group, 1.0), back, group))
                return carry

            lax.fori_loop(0, CHUNKS, step, 0)

        @pl.when(upper)
        def _():
            ours, theirs = lined(stat, group), lined(stat_x, group)
            keep = 1.0 / (1.0 + jnp.exp(theirs - ours))
            add = 1.0 / (1.0 + jnp.exp(ours - theirs))
            if group == 1:
                whole = (slot_lane // send) % CL_DEV == CL_DEV - 1
                keep, add = jnp.where(whole, 1.0, keep), jnp.where(whole, 0.0, add)

            def step(c, carry):
                finish(c, gather(chosen(c, group, keep), back, group) + gather(chosen(c, group, add), back_x, group))
                return carry

            lax.fori_loop(0, CHUNKS, step, 0)

    for group in range(2):
        for j in range(CL_DEV):
            sums = jnp.zeros((1, width), jnp.float32)
            final = (j, group) == (CL_DEV - 1, 1)
            if final:

                @pl.when(upper)
                def _():
                    def wait_lent(s, carry):
                        lend(half + s, s, s).wait_recv()
                        return carry

                    lax.fori_loop(0, half, wait_lent, 0)
                    k32 = lent[:, 0].reshape(span, width).astype(jnp.float32)
                    vacant = k32 > 0.5 * EMPTY
                    keys_x[...] = jnp.where(vacant, 0.0, k32).astype(jnp.bfloat16)
                    flags = dot_t(ones, jnp.where(vacant, 1.0, 0.0).astype(jnp.bfloat16))
                    bias_x[...] = jnp.where(flags > 0.5, LOW, 0.0)

            for b in range(zones):
                first, last, far = group * half + b * part, group * half + (b + 1) * part, (b + 1) * block

                def arrived(s, carry):
                    @pl.when(s != group * half + pos)
                    def _():
                        forward(j, s, s, base + s - group * half).wait_recv()

                    return carry

                lax.fori_loop(first, last, arrived, 0)
                q = recv[j, first:last, 0].reshape(block, width)
                k32 = recv[j, first:last, 1].reshape(block, width).astype(jnp.float32)
                vacant = k32 > 0.5 * EMPTY
                k32 = jnp.where(vacant, 0.0, k32)
                keys[b * block : far, :] = k32.astype(jnp.bfloat16)
                flags = dot_t(ones, jnp.where(vacant, 1.0, 0.0).astype(jnp.bfloat16))
                bias[:, b * block : far] = jnp.where(flags > 0.5, LOW, 0.0)
                scores = dot_t(q, keys[:far, :]) * scale + bias[0:1, :far]
                tail = scores[:, b * block :] + causal
                scores = tail if b == 0 else jnp.concatenate([scores[:, : b * block], tail], axis=1)
                v = recv[j, group * half : last, 2].reshape(far, width)

                def finish(scores, v):
                    highest = jnp.max(scores, axis=1, keepdims=True)
                    weights = jnp.exp(scores - highest)
                    total = jnp.sum(weights, axis=1, keepdims=True)
                    mixed = jnp.dot(weights.astype(jnp.bfloat16), v, preferred_element_type=jnp.float32)
                    att[j, first:last] = (mixed / total).astype(jnp.bfloat16).reshape(part, send, width)
                    parts[b * part : (b + 1) * part, j] = split(highest, total)

                if final:

                    @pl.when(upper)
                    def _():
                        more = dot_t(q, keys_x[...]) * scale + bias_x[0:1, :]
                        values = lent[:, 1].reshape(span, width)
                        finish(jnp.concatenate([more, scores], axis=1), jnp.concatenate([values, v], axis=0))

                    @pl.when(lower)
                    def _():
                        finish(scores, v)

                else:
                    finish(scores, v)
                unit = unit_rows(q.astype(jnp.float32)) + unit_rows(k32)
                sums = sums + jnp.sum(unit, axis=0, keepdims=True)

                def give(s, carry):
                    @pl.when(s != group * half + pos)
                    def _():
                        returned(j, s, group * half + pos, base + s - group * half).start()

                    return carry

                lax.fori_loop(first, last, give, 0)
            back[group * half + pos, j] = att[j, group * half + pos]
            held_sum[group, j : j + 1, :] = sums
            if final:
                continue

            @pl.when(lower)
            def _():
                for b in range(zones):
                    first, last = group * half + b * part, group * half + (b + 1) * part

                    def wait_ask(s, carry):
                        ask(j, s, s, half + s - group * half).wait_recv()
                        return carry

                    lax.fori_loop(first, last, wait_ask, 0)
                    q = asked[j, first:last].reshape(block, width)
                    scores = dot_t(q, keys[...]) * scale + bias[0:1, :]
                    highest = jnp.max(scores, axis=1, keepdims=True)
                    weights = jnp.exp(scores - highest)
                    total = jnp.sum(weights, axis=1, keepdims=True)
                    v = recv[j, group * half : (group + 1) * half, 2].reshape(span, width)
                    mixed = jnp.dot(weights.astype(jnp.bfloat16), v, preferred_element_type=jnp.float32)
                    att_x[j, first:last] = (mixed / total).astype(jnp.bfloat16).reshape(part, send, width)
                    parts_x[b * part : (b + 1) * part, j] = split(highest, total)

                    def give_x(s, carry):
                        answered(j, s, group * half + pos, half + s - group * half).start()
                        return carry

                    lax.fori_loop(first, last, give_x, 0)

        @pl.when(upper)
        def _():
            line_up(parts, told, group)

            def tell(s, carry):
                @pl.when(s != pos)
                def _():
                    noted(group * half + s, group * half + pos, half + s).start()

                return carry

            lax.fori_loop(0, half, tell, 0)
            stat[group * half + pos] = told[group * half + pos]

        @pl.when(lower)
        def _():
            line_up(parts_x, told_x, group)

            def tell(s, carry):
                noted_x(group * half + s, group * half + pos, half + s).start()
                return carry

            lax.fori_loop(0, half, tell, 0)

    other = 1 - side
    swap = pltpu.make_async_remote_copy(
        src_ref=held_sum.at[other], dst_ref=got_sum, send_sem=c_send, recv_sem=c_recv,
        device_id=(other * half + pos, head), device_id_type=MESH)
    swap.start()

    collect(0)
    collect(1)

    swap.wait()
    sums = held_sum[side] + got_sum[...]
    sums_ref[...] = sums
    keep_weight.wait()

    for i in range(1, heads):
        for c in range(CHUNKS):
            passed(i, c).wait()

    def settle(p, carry):
        for group in range(2):
            d = group * half + p

            @pl.when(p != pos)
            def _():
                for j in range(CL_DEV):
                    forward(j, d, group * half + pos, base + p).wait_send()
                    returned(j, d, group * half + pos, base + p).wait_send()

                @pl.when(upper)
                def _():
                    noted(d, group * half + pos, base + p).wait_send()

            @pl.when(upper)
            def _():
                for j in range(CL_DEV - group):
                    ask(j, d, group * half + pos, p).wait_send()

            @pl.when(lower)
            def _():
                for j in range(CL_DEV - group):
                    answered(j, d, group * half + pos, half + p).wait_send()
                if group == 1:
                    lend(d, pos, half + p).wait_send()
                noted_x(d, group * half + pos, half + p).wait_send()

        return carry

    lax.fori_loop(0, half, settle, 0)


def project_kernel(steps, joined_ref, weight_ref, sums_ref, out_hbm, cent_hbm, out, cent, sem):
    rows = joined_ref.shape[0] // steps
    sums = sums_ref[...]
    mean = jnp.mean(sums * sums, axis=-1, keepdims=True)
    cent[0] = sums * lax.rsqrt(mean + norm_eps)
    copies = [pltpu.make_async_copy(cent, cent_hbm, sem.at[steps])]
    copies[0].start()
    for i in range(steps):
        at = slice(i * rows, (i + 1) * rows)
        out[at] = jnp.dot(joined_ref[at], weight_ref[...], preferred_element_type=jnp.float32).astype(jnp.bfloat16)
        copy = pltpu.make_async_copy(out.at[at], out_hbm.at[at], sem.at[i])
        copy.start()
        copies.append(copy)
    for copy in copies:
        copy.wait()


def project(joined, weight, sums, steps):
    tokens, columns = joined.shape[0], weight.shape[1]
    return pl.pallas_call(
        functools.partial(project_kernel, steps),
        out_shape=(
            jax.ShapeDtypeStruct((tokens, columns), jnp.bfloat16),
            jax.ShapeDtypeStruct((1,) + sums.shape, jnp.float32),
        ),
        in_specs=[pl.BlockSpec(memory_space=pltpu.VMEM)] * 3,
        out_specs=(pl.BlockSpec(memory_space=pltpu.HBM),) * 2,
        scratch_shapes=[
            pltpu.VMEM((tokens, columns), jnp.bfloat16),
            pltpu.VMEM((1,) + sums.shape, jnp.float32),
            pltpu.SemaphoreType.DMA((steps + 1,)),
        ],
        compiler_params=pltpu.CompilerParams(vmem_limit_bytes=8000000),
        name="project",
    )(joined, weight, sums)


def shards(n, heads, queries, key_rows, value_rows, cluster_ids, out_weight):
    tokens, width = queries.shape[1], queries.shape[2]
    send = CAP // n
    half = n // 2
    bf16, f32 = jnp.bfloat16, jnp.float32
    dma = pltpu.SemaphoreType.DMA
    pinned = [pltpu.with_memory_space_constraint(x, pltpu.HBM)
              for x in (queries, key_rows, value_rows, cluster_ids[0, :, 0][None, :], out_weight)]
    joined, sums, weight = pl.pallas_call(
        functools.partial(kernel, n, heads, send),
        out_shape=(
            jax.ShapeDtypeStruct((tokens, heads * width), bf16),
            jax.ShapeDtypeStruct((CL_DEV, width), f32),
            jax.ShapeDtypeStruct(out_weight.shape, bf16),
        ),
        in_specs=[pl.BlockSpec(memory_space=pltpu.HBM)] * 5,
        out_specs=(pl.BlockSpec(memory_space=pltpu.VMEM),) * 3,
        scratch_shapes=[
            pltpu.VMEM((1, tokens), jnp.int32),
            pltpu.VMEM((tokens, 4 * width), bf16),
            pltpu.VMEM((CL_DEV, n, 3, send, width), bf16),
            pltpu.VMEM((CL_DEV, n, 3, send, width), bf16),
            pltpu.VMEM((CL_DEV, n, send, width), bf16),
            pltpu.VMEM((CL_DEV, n, send, width), bf16),
            pltpu.VMEM((CL_DEV, n, send, width), bf16),
            pltpu.VMEM((n, CL_DEV, send, width), bf16),
            pltpu.VMEM((n, CL_DEV, send, width), bf16),
            pltpu.VMEM((half, CL_DEV, send, width), bf16),
            pltpu.VMEM((half, CL_DEV, send, width), bf16),
            pltpu.VMEM((n, 1, 128), f32),
            pltpu.VMEM((n, 1, 128), f32),
            pltpu.VMEM((n, 1, 128), f32),
            pltpu.VMEM((n, 1, 128), f32),
            pltpu.VMEM((half, 2, send, width), bf16),
            pltpu.VMEM((half * send, width), bf16),
            pltpu.VMEM((8, half * send), f32),
            pltpu.VMEM((half * send, width), bf16),
            pltpu.VMEM((8, half * send), f32),
            pltpu.VMEM((tokens, 128), jnp.int32),
            pltpu.VMEM((2, CL_DEV, width), f32),
            pltpu.VMEM((CL_DEV, width), f32),
            pltpu.VMEM((tokens, width), f32),
            dma((5,)),
        ]
        + [dma((CL_DEV, n))] * 8
        + [dma((n,))] * 4
        + [dma((max(1, heads - 1), CHUNKS))] * 2
        + [dma, dma],
        compiler_params=pltpu.CompilerParams(
            collective_id=0, has_side_effects=True, vmem_limit_bytes=40000000
        ),
        name="route",
    )(*pinned)
    return project(joined, weight, sums, 4)


def solution(mesh):
    in_specs = (
        P("head", "ctx", None),
        P("head", "ctx", None),
        P("head", "ctx", None),
        P("head", "ctx", None),
        P(None, "head"),
    )
    out_specs = (P("ctx", "head"), P("head", "ctx", None))
    body = functools.partial(shards, mesh.shape["ctx"], mesh.shape["head"])
    return jax.shard_map(body, mesh=mesh, in_specs=in_specs, out_specs=out_specs, check_vma=False)
```
